512 devices in a mesh: section: 16 (over z, x_hi), expert: 32 (over x_lo, y, core).
Axes of the slice: x: 4 (x_hi: 2, x_lo: 2; x = x_hi * 2 + x_lo), y: 8, z: 8, core: 2. Of those that a mesh axis runs over, the one named last changes fastest.
Arguments:
- acts: bfloat16 [16, 4096, 3584], P('section', 'expert'), may hold values from -6 to 6
- expert_ids: int32 [16, 4096, 8], P('section', 'expert'), may hold values from 0 to 255, as said below
- gate_weights: bfloat16 [16, 4096, 8], P('section', 'expert'), may hold values from 0.049804688 to 0.34960938
- norm_gain: float32 [16, 3584], P('section'), may hold values from 0.5 to 1.5
- w_in: bfloat16 [16, 4096, 2, 3584], P('section', 'expert'), may hold values from -0.09375 to 0.09375
- w_out: bfloat16 [16, 4096, 3584], P('section', 'expert'), may hold values from -0.1875 to 0.1875
Outputs:
- advanced: bfloat16 [16, 4096, 3584], P('section', 'expert')
The draws below stay inside these ranges and needn't reach their ends.
Inputs may be any that keep to these rules, and one draw needn't show every extreme that they name: `expert_ids`: the 8 ids of a token are distinct. Of the 128 tokens of one device, at most 24 choose any one expert below 4, and one such expert is chosen by exactly 24.
All inputs are finite; a program needn't handle non-finite values.
Results may differ from the reference program's by a relative error of at most 0.0023.
Values may be sent and summed in bfloat16 or wider, within the bound.
A program may use at most 64 MiB of HBM per device.

```python
import jax
import jax.numpy as jnp
from jax import lax

D = 3584
HID = 1024
EXPERTS = 256
TOPK = 8
SLICES = 8
IN_FLIGHT = 4
TOK_DEV = 128
MB = 4096
N_SECTION = 16
N_EXPERT = 32


def device_block(key):
    flight = N_EXPERT // SLICES
    cap = 3 * TOK_DEV // 16
    first, second, third, fourth = jax.random.split(key, 4)
    ranking = jax.random.permutation(first, flight)
    counts = jnp.where(ranking == 0, cap, cap // 2)
    token_scores = jax.random.randint(second, (flight, TOK_DEV), 0, 65536) * TOK_DEV + jnp.arange(TOK_DEV, dtype=jnp.int32)[None, :]
    order = jnp.argsort(token_scores, axis=-1, stable=True)
    place = jnp.argsort(order, axis=-1, stable=True)
    hits = (place < counts[:, None]).T
    listed = jnp.sort(jnp.where(hits, jnp.arange(flight, dtype=jnp.int32)[None, :], EXPERTS), axis=-1)
    listed = jnp.concatenate([listed, jnp.full((TOK_DEV, TOPK - flight), EXPERTS, jnp.int32)], axis=-1)
    taken = jnp.sum(hits.astype(jnp.int32), axis=-1)
    others = EXPERTS - flight
    other_scores = jax.random.randint(third, (TOK_DEV, others), 0, 65536) * others + jnp.arange(others, dtype=jnp.int32)[None, :]
    outside = jnp.argsort(other_scores, axis=-1, stable=True)[:, :TOPK].astype(jnp.int32) + flight
    slots = jnp.arange(TOPK, dtype=jnp.int32)[None, :]
    merged = jnp.where(slots < taken[:, None], listed, outside)
    shuffle = jnp.argsort(jax.random.randint(fourth, (TOK_DEV, TOPK), 0, 65536) * TOPK + slots, axis=-1, stable=True)
    return jnp.take_along_axis(merged, shuffle, axis=-1).astype(jnp.int32)


def draw_expert_ids(key, part):
    keys = jax.random.split(jax.random.fold_in(key, 17), N_SECTION * N_EXPERT)
    blocks = jax.vmap(device_block)(keys)
    return blocks.reshape(N_SECTION, MB, TOPK).astype(jnp.int32)


def shard_levels(own_key, shape, cuts, smallest, largest):
    def one(dim, shards_of):
        heights = jax.random.uniform(jax.random.fold_in(jax.random.fold_in(own_key, 6), dim), (shards_of,), jnp.float32, smallest / len(cuts), largest / len(cuts))
        return jnp.repeat(jnp.exp(heights), shape[dim] // shards_of).reshape((-1,) + (1,) * (len(shape) - dim - 1))

    level = one(*cuts[0])
    for cut in cuts[1:]:
        level = level * one(*cut)
    return level


def noise(rng, dims, spread, most, shards=(), kind=jnp.bfloat16):
    array = spread * jax.random.normal(rng, dims, jnp.float32)
    if shards:
        array = array * shard_levels(rng, dims, shards, -0.22, 0.18)
    return jnp.clip(array, -most, most).astype(kind)


def setup_inputs(seed: int = 0) -> dict:
    key_of = jax.random.split(jax.random.key(seed), 7)
    return {
        "acts": noise(key_of[0], (N_SECTION, MB, D), 1.0, 6.0, ((0, 16), (1, 32))),
        "expert_ids": draw_expert_ids(jax.random.fold_in(key_of[6], 71), 0),
        "gate_weights": jnp.clip(0.049804688 + 0.2998047 * jax.random.uniform(key_of[2], (N_SECTION, MB, TOPK), jnp.float32) ** shard_levels(key_of[2], (N_SECTION, MB, TOPK), ((0, 16), (1, 32)), -0.2, 0.2), 0.049804688, 0.34960938).astype(jnp.bfloat16),
        "norm_gain": jnp.clip(1.0 + 0.1 * jax.random.normal(key_of[3], (N_SECTION, D), jnp.float32), 0.5, 1.5),
        "w_in": noise(key_of[4], (N_SECTION, IN_FLIGHT * HID, 2, D), D ** -0.5, 0.09375, ((0, 16), (1, 32))),
        "w_out": noise(key_of[5], (N_SECTION, IN_FLIGHT * HID, D), HID ** -0.5, 0.1875, ((0, 16), (1, 32))),
    }


def section_layer(x, ids, gw, gain, w_in, w_out):
    rows_all = N_EXPERT * (3 * TOK_DEV // 16)
    xf = x.astype(jnp.float32)
    normed = (xf * lax.rsqrt(lax.optimization_barrier(jnp.mean(xf * xf, axis=-1, keepdims=True)) + 1e-06) * gain).astype(jnp.bfloat16)
    gwf = gw.astype(jnp.float32)

    def per_expert(delta, expert):
        hit = ids == expert
        chosen = jnp.any(hit, axis=-1)
        weight = lax.optimization_barrier(jnp.sum(jnp.where(hit, gwf, jnp.float32(0.0)), axis=-1))
        index = jnp.nonzero(chosen, size=rows_all, fill_value=0)[0].astype(jnp.int32)
        valid = (jnp.arange(rows_all) < jnp.sum(chosen.astype(jnp.int32))).astype(jnp.float32)
        rows = normed[index].astype(jnp.float32)
        wrow = weight[index]
        start = (expert * HID).astype(jnp.int32)
        win = lax.dynamic_slice_in_dim(w_in, start, HID, 0).astype(jnp.float32)
        wout = lax.dynamic_slice_in_dim(w_out, start, HID, 0).astype(jnp.float32).reshape(SLICES, HID // SLICES, D)
        proj = jnp.einsum('rd,hgd->rhg', rows, win)
        hidden = (wrow[:, None] * jax.nn.silu(proj[:, :, 0]) * proj[:, :, 1]).astype(jnp.bfloat16)
        hidden = lax.optimization_barrier(hidden).astype(jnp.float32).reshape(rows_all, SLICES, HID // SLICES)
        parts = jnp.einsum('rsh,shd->rsd', hidden, wout).astype(jnp.bfloat16)
        parts = lax.optimization_barrier(parts).astype(jnp.float32)
        delta = delta.at[index].add(lax.optimization_barrier(jnp.sum(parts, axis=1)) * valid[:, None])
        return (delta, None)
    delta, _ = lax.scan(per_expert, jnp.zeros((MB, D), jnp.float32), jnp.arange(N_EXPERT // SLICES, dtype=jnp.int32))
    return (xf + delta).astype(jnp.bfloat16)

def reference(acts, expert_ids, gate_weights, norm_gain, w_in, w_out):
    outputs = lax.map(lambda item: section_layer(*item), (acts, expert_ids, gate_weights, norm_gain, w_in, w_out))
    return jnp.roll(outputs, 1, axis=0)
```

```python
import jax
import jax.numpy as jnp
from jax import lax
from jax.experimental import pallas as pl
from jax.experimental.pallas import tpu as pltpu
from jax.sharding import PartitionSpec as P

CAP = 24
RING = 8
HALF = 4
WIDE = 512
MESH = pl.DeviceIdType.MESH
BF = jnp.bfloat16
F32 = jnp.float32


def relay(
    acts, ids, gates, gain, w_in, w_out,
    out,
    win, wout, resid, table_out, table_in, normed,
    rows, cross, proj, hid, part, came, result,
    local_sem, w_send, w_recv, acts_send, acts_recv, table_send, table_recv,
    cross_send, cross_recv, out_send, out_recv,
    back_send, back_recv, last_send, last_recv,
):
    tok, width = acts.shape
    chunks = width // WIDE
    sec = lax.axis_index("section")
    me = lax.axis_index("expert")
    n_sec = lax.axis_size("section")
    x, y, core = me // 16, (me // 2) % RING, me % 2
    own = y // HALF
    r = y % HALF
    flip = (r >= 2).astype(jnp.int32)
    edge = jnp.logical_or(r == 0, r == 3)
    inner = jnp.logical_not(edge)
    up = 1 - 2 * flip
    far = 1 - own

    def at(col, row, c):
        return col * 16 + row * 2 + c

    def ring(step):
        return at(x, (y + step + RING) % RING, core)

    up_dev, down_dev = ring(up), ring(-up)
    across = at(1 - x, y, core)
    mate = at(x, y, 1 - core)
    after, before = (sec + 1) % n_sec, (sec + n_sec - 1) % n_sec

    def place(p):
        return (own * HALF + 3 * flip + up * p + 2 * RING) % RING

    barrier = pltpu.get_barrier_semaphore()
    partners = [
        (sec, up_dev), (sec, down_dev), (sec, across), (sec, mate),
        (after, me), (after, across), (before, me), (before, across),
    ]
    for who in partners:
        pl.semaphore_signal(barrier, inc=1, device_id=who, device_id_type=MESH)
    pl.semaphore_wait(barrier, len(partners))

    def remote(src, dst, send, recv, who):
        return pltpu.make_async_remote_copy(
            src_ref=src, dst_ref=dst, send_sem=send, recv_sem=recv,
            device_id=who, device_id_type=MESH,
        )

    own_in = pltpu.make_async_copy(w_in, win.at[core], local_sem.at[0])
    own_out = pltpu.make_async_copy(w_out, wout.at[core], local_sem.at[1])
    mate_in = remote(w_in, win.at[core], w_send.at[0], w_recv.at[0], (sec, mate))
    mate_out = remote(w_out, wout.at[core], w_send.at[1], w_recv.at[1], (sec, mate))
    keep = remote(acts, resid, acts_send, acts_recv, (after, me))

    chosen = ids[...]
    weight = gates[...].astype(F32)
    earlier = (
        lax.broadcasted_iota(jnp.int32, (tok, tok), 0)
        < lax.broadcasted_iota(jnp.int32, (tok, tok), 1)
    ).astype(BF)

    def slots(j):
        hit = chosen == j
        present = jnp.max(hit.astype(F32), axis=0, keepdims=True)
        amount = jnp.sum(jnp.where(hit, weight, 0.0), axis=0, keepdims=True)
        count = jnp.dot(
            jnp.broadcast_to(present, (8, tok)).astype(BF), earlier,
            preferred_element_type=F32,
        )[:1]
        index = lax.broadcasted_iota(jnp.int32, (CAP, tok), 0).astype(F32)
        taken = jnp.logical_and(index == count, present > 0.5)
        return taken.astype(F32), amount

    @pl.loop(0, tok // 16)
    def _(i):
        block = pl.ds(pl.multiple_of(i * 16, 16), 16)
        v = acts[block, :].astype(F32)
        mean = jnp.mean(v * v, axis=-1, keepdims=True)
        normed[block, :] = (v * lax.rsqrt(mean + 1e-06) * gain[...]).astype(BF)

    def gather(j, dst):
        pick = slots(j)[0].astype(BF)

        @pl.loop(0, chunks)
        def _(k):
            cols = pl.ds(pl.multiple_of(k * WIDE, WIDE), WIDE)
            dst[:, cols] = jnp.dot(
                pick, normed[:, cols], preferred_element_type=F32
            ).astype(BF)

    for h in range(2):
        gather(2 * (1 - x) + h, cross.at[h])
        remote(
            cross.at[h], rows.at[h, y, 1], cross_send.at[h], cross_recv.at[h],
            (sec, across),
        ).start()
    gather(2 * x + own, rows.at[own, y, 0])
    gather(2 * x + far, rows.at[far, y, 0])

    def push(h, p, i, upward):
        s = place(p)
        d = flip if upward else 1 - flip
        return remote(
            rows.at[h, s, i], rows.at[h, s, i], out_send.at[d, h, s, i],
            out_recv.at[h, s, i], (sec, up_dev if upward else down_dev),
        )

    def got(h, p, i):
        push(h, p, i, True).wait_recv()

    def first(i):
        @pl.when(edge)
        def _():
            push(own, 0, i, True).start()
            push(far, 0, i, False).start()

        @pl.when(inner)
        def _():
            push(own, 1, i, True).start()
            push(far, 1, i, False).start()
            push(own, 1, i, False).start()

    first(0)
    keep.start()
    own_in.start()
    own_out.start()
    mate_in.start()
    mate_out.start()
    for j in range(4):
        taken, amount = slots(j)
        table_out[j] = (taken * amount).astype(BF)
    table = remote(table_out, table_in, table_send, table_recv, (after, me))
    table.start()
    for h in range(2):
        remote(
            cross.at[h], rows.at[h, y, 1], cross_send.at[h], cross_recv.at[h],
            (sec, across),
        ).wait()
    first(1)

    @pl.when(edge)
    def _():
        for p in (7, 1, 6):
            for i in range(2):
                if p == 1:
                    got(far, 1, i)
                    push(far, 1, i, False).start()
                else:
                    got(own, p, i)
                    push(own, p, i, True).start()
        for p in range(1, 6):
            for i in range(2):
                got(own, p, i)

    @pl.when(inner)
    def _():
        for low, high in ((0, 2), (7, 3), (6, 4), (None, 5)):
            for i in range(2):
                if low is not None:
                    got(own, low, i)
                    push(own, low, i, True).start()
                got(own, high, i)
                push(own, high, i, False).start()

    own_in.wait()
    own_out.wait()
    mate_in.wait()
    mate_out.wait()
    total = RING * 2 * CAP

    proj[...] = jnp.zeros_like(proj)

    @pl.loop(0, chunks)
    def _(k):
        cols = pl.ds(pl.multiple_of(k * WIDE, WIDE), WIDE)
        block = rows[own, :, :, :, cols].reshape(total, WIDE)
        for c in range(2):
            proj[c] += lax.dot_general(
                block, win[c, :, cols], (((1,), (1,)), ((), ())),
                preferred_element_type=F32,
            )

    for c in range(2):
        g = proj[c, :, :128]
        u = proj[c, :, 128:]
        hid[:, :, :, c * 128:(c + 1) * 128] = (
            (jax.nn.silu(g) * u).astype(BF).reshape(RING, 2, CAP, 128)
        )

    def work(s):
        @pl.loop(0, chunks)
        def _(k):
            cols = pl.ds(pl.multiple_of(k * WIDE, WIDE), WIDE)
            both = wout[:, :, cols].reshape(256, WIDE)
            for i in range(2):
                part[s, i, :, cols] = jnp.dot(
                    hid[s, i], both, preferred_element_type=F32
                ).astype(BF)

    def back(src, h, p, i, upward):
        s = place(p)
        d = flip if upward else 1 - flip
        return remote(
            src, came.at[d, h, s, i], back_send.at[h, s, i], back_recv.at[d, h, s, i],
            (sec, up_dev if upward else down_dev),
        )

    def arrived(h, p, i, upward):
        s = place(p)
        d = flip if upward else 1 - flip
        box = came.at[d, h, s, i]
        back(box, h, p, i, upward).wait_recv()
        return box

    def add(p, i, box):
        s = place(p)

        @pl.loop(0, chunks)
        def _(k):
            cols = pl.ds(pl.multiple_of(k * WIDE, WIDE), WIDE)
            part[s, i, :, cols] = (
                part[s, i, :, cols].astype(F32) + box[:, cols].astype(F32)
            ).astype(BF)

    def merge(p, i, upward):
        add(p, i, arrived(own, p, i, upward))
        back(part.at[place(p), i], own, p, i, upward).start()

    def deliver(src, h, i):
        return remote(
            src, result.at[2 * x + h], last_send.at[h, i], last_recv.at[2 * x + h],
            (after, me if i == 0 else across),
        )

    @pl.loop(0, RING)
    def _(q):
        pos = (RING + 5 - q) % RING
        s = place(pos)
        work(s)

        @pl.when(jnp.logical_and(edge, jnp.logical_and(pos >= 1, pos <= 5)))
        def _():
            for i in range(2):
                back(part.at[s, i], own, pos, i, True).start()

    @pl.when(edge)
    def _():
        for i in range(2):
            merge(6, i, False)
        for i in range(2):
            merge(7, i, False)
        for i in range(2):
            box = arrived(far, 1, i, True)
            back(box, far, 1, i, True).start()
        for i in range(2):
            add(0, i, arrived(own, 0, i, False))
            deliver(part.at[place(0), i], own, i).start()
        for i in range(2):
            deliver(arrived(far, 0, i, True), far, i).start()

    @pl.when(inner)
    def _():
        for low, high in ((6, 5), (7, 4), (0, 3), (None, 2)):
            for i in range(2):
                merge(high, i, True)
                if low is not None:
                    merge(low, i, False)
        for i in range(2):
            add(1, i, arrived(own, 1, i, True))
            add(1, i, arrived(own, 1, i, False))
            deliver(part.at[place(1), i], own, i).start()
        for i in range(2):
            deliver(arrived(far, 1, i, True), far, i).start()

    keep.wait()
    table.wait()
    for j in range(4):
        remote(
            result.at[j], result.at[j], last_send.at[0, 0], last_recv.at[j], (after, me)
        ).wait_recv()

    @pl.loop(0, chunks)
    def _(k):
        cols = pl.ds(pl.multiple_of(k * WIDE, WIDE), WIDE)
        total = resid[:, cols].astype(F32)
        for j in range(4):
            total += lax.dot_general(
                table_in[j], result[j, :, cols], (((0,), (0,)), ((), ())),
                preferred_element_type=F32,
            )
        out[:, cols] = total.astype(BF)

    for i in range(2):
        @pl.when(edge)
        def _():
            push(own, 0, i, True).wait_send()
            push(far, 0, i, False).wait_send()
            for p in (7, 6):
                push(own, p, i, True).wait_send()
            push(far, 1, i, False).wait_send()
            for p in (1, 2, 3, 4, 5):
                back(part.at[0, 0], own, p, i, True).wait_send()
            for p in (6, 7):
                back(part.at[0, 0], own, p, i, False).wait_send()
            back(part.at[0, 0], far, 1, i, True).wait_send()

        @pl.when(inner)
        def _():
            push(own, 1, i, True).wait_send()
            push(far, 1, i, False).wait_send()
            push(own, 1, i, False).wait_send()
            for p in (0, 7, 6):
                push(own, p, i, True).wait_send()
                back(part.at[0, 0], own, p, i, False).wait_send()
            for p in (2, 3, 4, 5):
                push(own, p, i, False).wait_send()
                back(part.at[0, 0], own, p, i, True).wait_send()

        for h in range(2):
            deliver(part.at[0, 0], h, i).wait_send()


def local(acts, expert_ids, gate_weights, norm_gain, w_in, w_out):
    tok, width = acts.shape[1:]
    hid = w_out.shape[1]
    vmem = pl.BlockSpec(memory_space=pltpu.VMEM)
    hbm = pl.BlockSpec(memory_space=pl.ANY)
    dma = pltpu.SemaphoreType.DMA
    flat_in = w_in[0].transpose(1, 0, 2).reshape(2 * hid, width)
    moved = pl.pallas_call(
        relay,
        out_shape=jax.ShapeDtypeStruct((tok, width), BF),
        in_specs=[vmem, vmem, vmem, vmem, hbm, hbm],
        out_specs=vmem,
        scratch_shapes=[
            pltpu.VMEM((2, 2 * hid, width), BF),
            pltpu.VMEM((2, hid, width), BF),
            pltpu.VMEM((tok, width), BF),
            pltpu.VMEM((4, CAP, tok), BF),
            pltpu.VMEM((4, CAP, tok), BF),
            pltpu.VMEM((tok, width), BF),
            pltpu.VMEM((2, RING, 2, CAP, width), BF),
            pltpu.VMEM((2, CAP, width), BF),
            pltpu.VMEM((2, RING * 2 * CAP, 2 * hid), F32),
            pltpu.VMEM((RING, 2, CAP, 2 * hid), BF),
            pltpu.VMEM((RING, 2, CAP, width), BF),
            pltpu.VMEM((2, 2, RING, 2, CAP, width), BF),
            pltpu.VMEM((4, CAP, width), BF),
            dma((2,)), dma((2,)), dma((2,)), dma, dma, dma, dma,
            dma((2,)), dma((2,)), dma((2, 2, RING, 2)), dma((2, RING, 2)),
            dma((2, RING, 2)), dma((2, 2, RING, 2)), dma((2, 2)), dma((4,)),
        ],
        compiler_params=pltpu.CompilerParams(
            collective_id=0, has_side_effects=True, vmem_limit_bytes=60 * 2**20
        ),
    )(acts[0], expert_ids[0].T, gate_weights[0].T, norm_gain, flat_in, w_out[0])
    return moved[None]


def solution(mesh):
    placed = (
        P("section", "expert", None),
        P("section", "expert", None),
        P("section", "expert", None),
        P("section", None),
        P("section", "expert", None, None),
        P("section", "expert", None),
    )
    return jax.shard_map(
        local, mesh=mesh, in_specs=placed, out_specs=P("section", "expert", None), check_vma=False
    )
```

```python
import jax
import jax.numpy as jnp
from jax import lax
from jax.experimental import pallas as pl
from jax.experimental.pallas import tpu as pltpu
from jax.sharding import PartitionSpec as P

CAP = 24
RING = 8
HALF = 4
WIDE = 512
MESH = pl.DeviceIdType.MESH
BF = jnp.bfloat16
F32 = jnp.float32
SEND, WORK, ADD, BACK, LAST = range(5)
EDGE = (
    (0, 0, 0, 0, 1), (0, 1, 0, 0, -1), (1, 0, 0, 0, 0), (1, 0, 1, 0, 0), (0, 0, 7, 0, 1),
    (0, 1, 0, 1, -1), (0, 0, 0, 1, 1), (1, 0, 7, 0, 0), (0, 1, 1, 0, -1), (1, 0, 0, 1, 0),
    (0, 0, 6, 0, 1), (0, 1, 1, 1, -1), (1, 0, 6, 0, 0), (0, 0, 7, 1, 1), (1, 0, 7, 1, 0),
    (0, 0, 6, 1, 1), (1, 0, 3, 0, 0), (1, 0, 6, 1, 0), (3, 0, 3, 0, 1), (1, 0, 2, 0, 0),
    (1, 0, 4, 0, 0), (3, 0, 2, 0, 1), (1, 0, 3, 1, 0), (3, 0, 4, 0, 1), (1, 0, 5, 0, 0),
    (3, 0, 5, 0, 1), (1, 0, 4, 1, 0), (3, 0, 4, 1, 1), (1, 0, 5, 1, 0), (3, 0, 5, 1, 1),
    (1, 0, 2, 1, 0), (3, 0, 3, 1, 1), (1, 0, 1, 1, 0), (3, 0, 2, 1, 1), (2, 0, 0, 0, 1),
    (3, 0, 1, 0, 1), (4, 0, 0, 0, 0), (2, 0, 6, 0, 1), (3, 0, 1, 1, 1), (3, 0, 6, 0, -1),
    (2, 0, 7, 0, 1), (3, 0, 7, 0, -1), (4, 1, 0, 0, 0), (2, 0, 6, 1, 1), (3, 0, 6, 1, -1),
    (3, 1, 1, 0, 1), (2, 0, 7, 1, 1), (3, 0, 7, 1, -1), (3, 1, 1, 1, 1), (2, 0, 0, 1, 1),
    (4, 0, 0, 1, 0), (4, 1, 0, 1, 0),
)
INNER = (
    (0, 0, 1, 0, 1), (0, 0, 1, 0, -1), (0, 1, 1, 0, -1), (1, 0, 1, 0, 0), (0, 0, 0, 0, 1),
    (1, 0, 0, 0, 0), (0, 1, 1, 1, -1), (0, 0, 1, 1, 1), (1, 0, 2, 0, 0), (1, 0, 1, 1, 0),
    (0, 0, 3, 0, -1), (0, 0, 7, 0, 1), (0, 0, 2, 0, -1), (1, 0, 3, 0, 0), (0, 0, 0, 1, 1),
    (1, 0, 7, 0, 0), (0, 0, 4, 0, -1), (0, 0, 6, 0, 1), (1, 0, 4, 0, 0), (1, 0, 6, 0, 0),
    (0, 0, 3, 1, -1), (0, 0, 7, 1, 1), (1, 0, 3, 1, 0), (0, 0, 5, 0, -1), (0, 0, 6, 1, 1),
    (1, 0, 5, 0, 0), (1, 0, 6, 1, 0), (0, 0, 4, 1, -1), (2, 0, 3, 0, 1), (1, 0, 4, 1, 0),
    (3, 0, 3, 0, 1), (0, 0, 5, 1, -1), (2, 0, 2, 0, 1), (1, 0, 5, 1, 0), (3, 0, 2, 0, 1),
    (0, 0, 2, 1, -1), (1, 0, 7, 1, 0), (0, 0, 1, 1, -1), (2, 0, 4, 0, 1), (3, 0, 4, 0, 1),
    (2, 0, 0, 0, 1), (1, 0, 2, 1, 0), (3, 0, 0, 0, -1), (2, 0, 5, 0, 1), (1, 0, 0, 1, 0),
    (3, 0, 5, 0, 1), (2, 0, 4, 1, 1), (2, 0, 7, 0, 1), (3, 0, 4, 1, 1), (2, 0, 5, 1, 1),
    (2, 0, 6, 0, 1), (3, 0, 5, 1, 1), (3, 0, 6, 0, -1), (3, 0, 7, 0, -1), (2, 0, 3, 1, 1),
    (2, 0, 7, 1, 1), (3, 0, 3, 1, 1), (2, 0, 2, 1, 1), (2, 0, 6, 1, 1), (3, 0, 2, 1, 1),
    (3, 0, 6, 1, -1), (3, 0, 7, 1, -1), (2, 0, 1, 0, 2), (4, 0, 1, 0, 0), (2, 0, 0, 1, 1),
    (3, 0, 0, 1, -1), (2, 0, 1, 1, 2), (4, 0, 1, 1, 0), (4, 1, 1, 0, 0), (4, 1, 1, 1, 0),
)


def relay(
    acts, ids, gates, gain, w_in, w_out,
    out,
    win, wout, resid, table_out, table_in, normed,
    rows, cross, part, came, result,
    local_sem, w_send, w_recv, acts_send, acts_recv, table_send, table_recv,
    cross_send, cross_recv, out_send, out_recv,
    back_send, back_recv, last_send, last_recv,
):
    tok, width = acts.shape
    chunks = width // WIDE
    sec = lax.axis_index("section")
    me = lax.axis_index("expert")
    n_sec = lax.axis_size("section")
    x, y, core = me // 16, (me // 2) % RING, me % 2
    own = y // HALF
    r = y % HALF
    flip = (r >= 2).astype(jnp.int32)
    edge = jnp.logical_or(r == 0, r == 3)
    inner = jnp.logical_not(edge)
    up = 1 - 2 * flip
    far = 1 - own

    def at(col, row, c):
        return col * 16 + row * 2 + c

    def ring(step):
        return at(x, (y + step + RING) % RING, core)

    up_dev, down_dev = ring(up), ring(-up)
    across = at(1 - x, y, core)
    mate = at(x, y, 1 - core)
    after, before = (sec + 1) % n_sec, (sec + n_sec - 1) % n_sec

    def place(p):
        return (own * HALF + 3 * flip + up * p + 2 * RING) % RING

    barrier = pltpu.get_barrier_semaphore()
    partners = [
        (sec, up_dev), (sec, down_dev), (sec, across), (sec, mate),
        (after, me), (after, across), (before, me), (before, across),
    ]
    for who in partners:
        pl.semaphore_signal(barrier, inc=1, device_id=who, device_id_type=MESH)
    pl.semaphore_wait(barrier, len(partners))

    def remote(src, dst, send, recv, who):
        return pltpu.make_async_remote_copy(
            src_ref=src, dst_ref=dst, send_sem=send, recv_sem=recv,
            device_id=who, device_id_type=MESH,
        )

    own_in = pltpu.make_async_copy(w_in, win.at[core], local_sem.at[0])
    own_out = pltpu.make_async_copy(w_out, wout.at[core], local_sem.at[1])
    mate_in = remote(w_in, win.at[core], w_send.at[0], w_recv.at[0], (sec, mate))
    mate_out = remote(w_out, wout.at[core], w_send.at[1], w_recv.at[1], (sec, mate))
    keep = remote(acts, resid, acts_send, acts_recv, (after, me))

    chosen = ids[...]
    weight = gates[...].astype(F32)
    earlier = (
        lax.broadcasted_iota(jnp.int32, (tok, tok), 0)
        < lax.broadcasted_iota(jnp.int32, (tok, tok), 1)
    ).astype(BF)

    def slots(j):
        hit = chosen == j
        present = jnp.max(hit.astype(F32), axis=0, keepdims=True)
        amount = jnp.sum(jnp.where(hit, weight, 0.0), axis=0, keepdims=True)
        count = jnp.dot(
            jnp.broadcast_to(present, (8, tok)).astype(BF), earlier,
            preferred_element_type=F32,
        )[:1]
        index = lax.broadcasted_iota(jnp.int32, (CAP, tok), 0).astype(F32)
        taken = jnp.logical_and(index == count, present > 0.5)
        return taken.astype(F32), amount

    @pl.loop(0, tok // 16)
    def _(i):
        block = pl.ds(pl.multiple_of(i * 16, 16), 16)
        v = acts[block, :].astype(F32)
        mean = jnp.mean(v * v, axis=-1, keepdims=True)
        normed[block, :] = (v * lax.rsqrt(mean + 1e-06) * gain[...]).astype(BF)

    def gather(j, dst):
        pick = slots(j)[0].astype(BF)

        @pl.loop(0, chunks)
        def _(k):
            cols = pl.ds(pl.multiple_of(k * WIDE, WIDE), WIDE)
            dst[:, cols] = jnp.dot(
                pick, normed[:, cols], preferred_element_type=F32
            ).astype(BF)

    def push(h, p, i, upward):
        s = place(p)
        d = flip if upward else 1 - flip
        return remote(
            rows.at[h, s, i], rows.at[h, s, i], out_send.at[d, h, s, i],
            out_recv.at[h, s, i], (sec, up_dev if upward else down_dev),
        )

    def back(src, h, p, i, upward):
        s = place(p)
        d = flip if upward else 1 - flip
        return remote(
            src, came.at[d, h, s, i], back_send.at[h, s, i], back_recv.at[d, h, s, i],
            (sec, up_dev if upward else down_dev),
        )

    def crossing(h):
        return remote(
            cross.at[h], rows.at[h, y, 1], cross_send.at[h], cross_recv.at[h], (sec, across)
        )

    def deliver(src, h, i):
        return remote(
            src, result.at[2 * x + h], last_send.at[h, i], last_recv.at[2 * x + h],
            (after, me if i == 0 else across),
        )

    def work(s, i):
        def step(k, acc):
            cols = pl.ds(pl.multiple_of(k * WIDE, WIDE), WIDE)
            block = rows[own, s, i, :, cols]
            return tuple(
                acc[c] + lax.dot_general(
                    block, win[c, :, cols], (((1,), (1,)), ((), ())),
                    preferred_element_type=F32,
                )
                for c in range(2)
            )

        zero = jnp.zeros((CAP, 256), F32)
        both = lax.fori_loop(0, chunks, step, (zero, zero))
        hid = jnp.concatenate(
            [(jax.nn.silu(v[:, :128]) * v[:, 128:]).astype(BF) for v in both], axis=1
        )

        @pl.loop(0, chunks)
        def _(k):
            cols = pl.ds(pl.multiple_of(k * WIDE, WIDE), WIDE)
            part[s, i, :, cols] = jnp.dot(
                hid, wout[:, :, cols].reshape(256, WIDE), preferred_element_type=F32
            ).astype(BF)

    def add(s, i, boxes):
        @pl.loop(0, chunks)
        def _(k):
            cols = pl.ds(pl.multiple_of(k * WIDE, WIDE), WIDE)
            total = part[s, i, :, cols].astype(F32)
            for box in boxes:
                total += box[:, cols].astype(F32)
            part[s, i, :, cols] = total.astype(BF)

    sides = (own, far)

    def run(role, ops):
        seen, weights = {(h, role, 0) for h in range(2)}, []

        def need(h, p, i):
            if (h, p, i) in seen:
                return
            seen.add((h, p, i))
            if p == role:
                crossing(sides[h]).wait_recv()
                if {(0, role, 1), (1, role, 1)} <= seen:
                    keep.start()
            else:
                push(sides[h], p, i, True).wait_recv()

        def box(h, p, i, upward):
            d = flip if upward else 1 - flip
            where = came.at[d, sides[h], place(p), i]
            back(where, sides[h], p, i, upward).wait_recv()
            return where

        for kind, h, p, i, way in ops:
            s = place(p)
            if kind == SEND:
                need(h, p, i)
                push(sides[h], p, i, way > 0).start()
            elif kind == WORK:
                need(h, p, i)
                if not weights:
                    weights.append(1)
                    for copy in (own_in, own_out, mate_in, mate_out):
                        copy.wait()
                work(s, i)
            elif kind == ADD:
                if role == 0:
                    ways = [False]
                elif p == 1:
                    ways = [False, True]
                else:
                    ways = [p in (2, 3, 4, 5)]
                add(s, i, [box(h, p, i, w) for w in ways])
            elif kind == BACK:
                src = box(h, p, i, True) if h == 1 else part.at[s, i]
                back(src, sides[h], p, i, way > 0).start()
            else:
                src = box(h, p, i, True) if h == 1 else part.at[s, i]
                deliver(src, sides[h], i).start()
        for kind, h, p, i, way in ops:
            if kind == SEND:
                push(sides[h], p, i, way > 0).wait_send()
            elif kind == BACK:
                back(part.at[0, 0], sides[h], p, i, way > 0).wait_send()
            elif kind == LAST:
                deliver(part.at[0, 0], sides[h], i).wait_send()

    for h in range(2):
        gather(2 * (1 - x) + h, cross.at[h])
        crossing(h).start()
    gather(2 * x + own, rows.at[own, y, 0])
    gather(2 * x + far, rows.at[far, y, 0])
    for j in range(4):
        taken, amount = slots(j)
        table_out[j] = (taken * amount).astype(BF)
    table = remote(table_out, table_in, table_send, table_recv, (after, me))
    table.start()
    own_in.start()
    own_out.start()
    mate_in.start()
    mate_out.start()

    @pl.when(edge)
    def _():
        run(0, EDGE)

    @pl.when(inner)
    def _():
        run(1, INNER)

    keep.wait()
    table.wait()
    for j in range(4):
        remote(
            result.at[j], result.at[j], last_send.at[0, 0], last_recv.at[j], (after, me)
        ).wait_recv()

    @pl.loop(0, chunks)
    def _(k):
        cols = pl.ds(pl.multiple_of(k * WIDE, WIDE), WIDE)
        total = resid[:, cols].astype(F32)
        for j in range(4):
            total += lax.dot_general(
                table_in[j], result[j, :, cols], (((0,), (0,)), ((), ())),
                preferred_element_type=F32,
            )
        out[:, cols] = total.astype(BF)

    for h in range(2):
        crossing(h).wait_send()


def local(acts, expert_ids, gate_weights, norm_gain, w_in, w_out):
    tok, width = acts.shape[1:]
    hid = w_out.shape[1]
    vmem = pl.BlockSpec(memory_space=pltpu.VMEM)
    hbm = pl.BlockSpec(memory_space=pl.ANY)
    dma = pltpu.SemaphoreType.DMA
    flat_in = w_in[0].transpose(1, 0, 2).reshape(2 * hid, width)
    moved = pl.pallas_call(
        relay,
        out_shape=jax.ShapeDtypeStruct((tok, width), BF),
        in_specs=[vmem, vmem, vmem, vmem, hbm, hbm],
        out_specs=vmem,
        scratch_shapes=[
            pltpu.VMEM((2, 2 * hid, width), BF),
            pltpu.VMEM((2, hid, width), BF),
            pltpu.VMEM((tok, width), BF),
            pltpu.VMEM((4, CAP, tok), BF),
            pltpu.VMEM((4, CAP, tok), BF),
            pltpu.VMEM((tok, width), BF),
            pltpu.VMEM((2, RING, 2, CAP, width), BF),
            pltpu.VMEM((2, CAP, width), BF),
            pltpu.VMEM((RING, 2, CAP, width), BF),
            pltpu.VMEM((2, 2, RING, 2, CAP, width), BF),
            pltpu.VMEM((4, CAP, width), BF),
            dma((2,)), dma((2,)), dma((2,)), dma, dma, dma, dma,
            dma((2,)), dma((2,)), dma((2, 2, RING, 2)), dma((2, RING, 2)),
            dma((2, RING, 2)), dma((2, 2, RING, 2)), dma((2, 2)), dma((4,)),
        ],
        compiler_params=pltpu.CompilerParams(
            collective_id=0, has_side_effects=True, vmem_limit_bytes=60 * 2**20
        ),
    )(acts[0], expert_ids[0].T, gate_weights[0].T, norm_gain, flat_in, w_out[0])
    return moved[None]


def solution(mesh):
    placed = (
        P("section", "expert", None),
        P("section", "expert", None),
        P("section", "expert", None),
        P("section", None),
        P("section", "expert", None, None),
        P("section", "expert", None),
    )
    return jax.shard_map(
        local, mesh=mesh, in_specs=placed, out_specs=P("section", "expert", None), check_vma=False
    )
```

```python
import jax
import jax.numpy as jnp
from jax import lax
from jax.experimental import pallas as pl
from jax.experimental.pallas import tpu as pltpu
from jax.sharding import PartitionSpec as P

CAP = 24
RING = 8
HALF = 4
WIDE = 512
HUGE = 1792
MESH = pl.DeviceIdType.MESH
BF = jnp.bfloat16
F32 = jnp.float32
SEND, WORK, ADD, BACK, LAST = range(5)
EDGE = (
    (0, 0, 0, 0, 1), (0, 1, 0, 0, -1), (0, 1, 1, 0, -1), (0, 0, 7, 0, 1), (1, 0, 0, 0, 0),
    (0, 0, 0, 1, 1), (1, 0, 7, 0, 0), (1, 0, 1, 0, 0), (0, 1, 0, 1, -1), (0, 0, 6, 0, 1),
    (1, 0, 6, 0, 0), (1, 0, 2, 0, 0), (0, 0, 7, 1, 1), (1, 0, 7, 1, 0), (0, 1, 1, 1, -1),
    (3, 0, 1, 0, 1), (1, 0, 0, 1, 0), (1, 0, 2, 1, 0), (0, 0, 6, 1, 1), (1, 0, 6, 1, 0),
    (3, 0, 2, 1, 1), (1, 0, 3, 0, 0), (1, 0, 4, 0, 0), (3, 0, 4, 0, 1), (1, 0, 5, 0, 0),
    (3, 0, 5, 0, 1), (1, 0, 1, 1, 0), (3, 0, 1, 1, 1), (1, 0, 3, 1, 0), (3, 0, 3, 1, 1),
    (1, 0, 5, 1, 0), (3, 0, 5, 1, 1), (1, 0, 4, 1, 0), (3, 0, 4, 1, 1), (3, 0, 3, 0, 1),
    (2, 0, 7, 0, 1), (3, 0, 7, 0, -1), (3, 0, 2, 0, 1), (2, 0, 6, 0, 1), (3, 0, 6, 0, -1),
    (4, 1, 0, 0, 0), (2, 0, 0, 1, 1), (4, 0, 0, 1, 0), (3, 1, 1, 0, 1), (2, 0, 6, 1, 1),
    (3, 0, 6, 1, -1), (2, 0, 7, 1, 1), (3, 0, 7, 1, -1), (3, 1, 1, 1, 1), (2, 0, 0, 0, 1),
    (4, 0, 0, 0, 0), (4, 1, 0, 1, 0),
)
INNER = (
    (0, 0, 1, 0, 1), (0, 1, 1, 0, -1), (0, 0, 1, 0, -1), (0, 0, 0, 0, 1), (0, 0, 2, 0, -1),
    (1, 0, 1, 0, 0), (0, 0, 1, 1, 1), (1, 0, 0, 0, 0), (1, 0, 1, 1, 0), (0, 1, 1, 1, -1),
    (0, 0, 7, 0, 1), (1, 0, 7, 0, 0), (1, 0, 2, 0, 0), (0, 0, 2, 1, -1), (0, 0, 0, 1, 1),
    (1, 0, 0, 1, 0), (0, 0, 3, 0, -1), (1, 0, 2, 1, 0), (0, 0, 6, 0, 1), (0, 0, 4, 0, -1),
    (1, 0, 6, 0, 0), (1, 0, 4, 0, 0), (0, 0, 7, 1, 1), (1, 0, 7, 1, 0), (1, 0, 3, 2, 0),
    (0, 0, 5, 0, -1), (0, 0, 1, 1, -1), (1, 0, 5, 0, 0), (0, 0, 6, 1, 1), (1, 0, 6, 1, 0),
    (0, 0, 3, 1, -1), (1, 0, 4, 1, 0), (2, 0, 2, 1, 1), (3, 0, 2, 1, 1), (0, 0, 5, 1, -1),
    (1, 0, 5, 1, 0), (2, 0, 4, 0, 1), (3, 0, 4, 0, 1), (0, 0, 4, 1, -1), (2, 0, 5, 0, 1),
    (3, 0, 5, 0, 1), (2, 0, 7, 0, 1), (3, 0, 7, 0, -1), (2, 0, 1, 1, 2), (4, 0, 1, 1, 0),
    (2, 0, 6, 0, 1), (3, 0, 6, 0, -1), (2, 0, 3, 1, 1), (3, 0, 3, 1, 1), (2, 0, 5, 1, 1),
    (3, 0, 5, 1, 1), (2, 0, 0, 1, 1), (3, 0, 0, 1, -1), (2, 0, 4, 1, 1), (3, 0, 4, 1, 1),
    (2, 0, 6, 1, 1), (3, 0, 6, 1, -1), (2, 0, 3, 0, 1), (3, 0, 3, 0, 1), (2, 0, 7, 1, 1),
    (3, 0, 7, 1, -1), (2, 0, 2, 0, 1), (3, 0, 2, 0, 1), (2, 0, 0, 0, 1), (3, 0, 0, 0, -1),
    (4, 1, 1, 0, 0), (2, 0, 1, 0, 2), (4, 0, 1, 0, 0), (4, 1, 1, 1, 0),
)


def relay(
    acts, ids, gates, gain, w_in, w_out,
    out,
    win, wout, resid, table_out, table_in, normed,
    rows, cross, part, came, result,
    local_sem, w_send, w_recv, acts_send, acts_recv, table_send, table_recv,
    cross_send, cross_recv, out_send, out_recv,
    back_send, back_recv, last_send, last_recv,
):
    tok, width = acts.shape
    chunks = width // WIDE
    sec = lax.axis_index("section")
    me = lax.axis_index("expert")
    n_sec = lax.axis_size("section")
    x, y, core = me // 16, (me // 2) % RING, me % 2
    own = y // HALF
    r = y % HALF
    flip = (r >= 2).astype(jnp.int32)
    edge = jnp.logical_or(r == 0, r == 3)
    inner = jnp.logical_not(edge)
    up = 1 - 2 * flip
    far = 1 - own

    def at(col, row, c):
        return col * 16 + row * 2 + c

    def ring(step):
        return at(x, (y + step + RING) % RING, core)

    up_dev, down_dev = ring(up), ring(-up)
    across = at(1 - x, y, core)
    mate = at(x, y, 1 - core)
    after, before = (sec + 1) % n_sec, (sec + n_sec - 1) % n_sec

    def place(p):
        return (own * HALF + 3 * flip + up * p + 2 * RING) % RING

    barrier = pltpu.get_barrier_semaphore()
    partners = [
        (sec, up_dev), (sec, down_dev), (sec, across), (sec, mate),
        (after, me), (after, across), (before, me), (before, across),
    ]
    for who in partners:
        pl.semaphore_signal(barrier, inc=1, device_id=who, device_id_type=MESH)

    def remote(src, dst, send, recv, who):
        return pltpu.make_async_remote_copy(
            src_ref=src, dst_ref=dst, send_sem=send, recv_sem=recv,
            device_id=who, device_id_type=MESH,
        )

    own_in = pltpu.make_async_copy(w_in, win.at[core], local_sem.at[0])
    own_out = pltpu.make_async_copy(w_out, wout.at[core], local_sem.at[1])
    mate_in = remote(w_in, win.at[core], w_send.at[0], w_recv.at[0], (sec, mate))
    mate_out = remote(w_out, wout.at[core], w_send.at[1], w_recv.at[1], (sec, mate))
    keep = remote(acts, resid, acts_send, acts_recv, (after, me))

    chosen = ids[...]
    weight = gates[...].astype(F32)
    earlier = (
        lax.broadcasted_iota(jnp.int32, (tok, tok), 0)
        < lax.broadcasted_iota(jnp.int32, (tok, tok), 1)
    ).astype(BF)

    def slots(j):
        hit = chosen == j
        present = jnp.max(hit.astype(F32), axis=0, keepdims=True)
        amount = jnp.sum(jnp.where(hit, weight, 0.0), axis=0, keepdims=True)
        count = jnp.dot(
            jnp.broadcast_to(present, (8, tok)).astype(BF), earlier,
            preferred_element_type=F32,
        )[:1]
        index = lax.broadcasted_iota(jnp.int32, (CAP, tok), 0).astype(F32)
        taken = jnp.logical_and(index == count, present > 0.5)
        return taken.astype(F32), amount

    @pl.loop(0, tok // 16)
    def _(i):
        block = pl.ds(pl.multiple_of(i * 16, 16), 16)
        v = acts[block, :].astype(F32)
        mean = jnp.mean(v * v, axis=-1, keepdims=True)
        normed[block, :] = (v * lax.rsqrt(mean + 1e-06) * gain[...]).astype(BF)

    def gather(j, dst):
        pick = slots(j)[0].astype(BF)

        @pl.loop(0, chunks)
        def _(k):
            cols = pl.ds(pl.multiple_of(k * WIDE, WIDE), WIDE)
            dst[:, cols] = jnp.dot(
                pick, normed[:, cols], preferred_element_type=F32
            ).astype(BF)

    def push(h, p, i, upward):
        s = place(p)
        d = flip if upward else 1 - flip
        return remote(
            rows.at[h, s, i], rows.at[h, s, i], out_send.at[d, h, s, i],
            out_recv.at[h, s, i], (sec, up_dev if upward else down_dev),
        )

    def back(src, h, p, i, upward):
        s = place(p)
        d = flip if upward else 1 - flip
        return remote(
            src, came.at[d, h, s, i], back_send.at[h, s, i], back_recv.at[d, h, s, i],
            (sec, up_dev if upward else down_dev),
        )

    def crossing(h):
        return remote(
            cross.at[h], rows.at[h, y, 1], cross_send.at[h], cross_recv.at[h], (sec, across)
        )

    def deliver(src, h, i):
        return remote(
            src, result.at[2 * x + h], last_send.at[h, i], last_recv.at[2 * x + h],
            (after, me if i == 0 else across),
        )

    def work(s, first, count):
        def step(k, acc):
            cols = pl.ds(pl.multiple_of(k * HUGE, HUGE), HUGE)
            block = rows[own, s, first:first + count, :, cols].reshape(count * CAP, HUGE)
            return tuple(
                acc[c] + lax.dot_general(
                    block, win[c, :, cols], (((1,), (1,)), ((), ())),
                    preferred_element_type=F32,
                )
                for c in range(2)
            )

        zero = jnp.zeros((count * CAP, 256), F32)
        both = lax.fori_loop(0, width // HUGE, step, (zero, zero))
        hid = jnp.concatenate(
            [(jax.nn.silu(v[:, :128]) * v[:, 128:]).astype(BF) for v in both], axis=1
        )

        @pl.loop(0, width // HUGE)
        def _(k):
            cols = pl.ds(pl.multiple_of(k * HUGE, HUGE), HUGE)
            part[s, first:first + count, :, cols] = jnp.dot(
                hid, wout[:, :, cols].reshape(256, HUGE), preferred_element_type=F32
            ).astype(BF).reshape(count, CAP, HUGE)

    def add(s, i, boxes):
        @pl.loop(0, chunks)
        def _(k):
            cols = pl.ds(pl.multiple_of(k * WIDE, WIDE), WIDE)
            total = part[s, i, :, cols].astype(F32)
            for box in boxes:
                total += box[:, cols].astype(F32)
            part[s, i, :, cols] = total.astype(BF)

    sides = (own, far)

    def run(role, ops):
        seen, weights = {(h, role, 0) for h in range(2)}, []

        def need(h, p, i):
            if (h, p, i) in seen:
                return
            seen.add((h, p, i))
            if p == role:
                crossing(sides[h]).wait_recv()
                if {(0, role, 1), (1, role, 1)} <= seen:
                    keep.start()
                    table.start()
            else:
                push(sides[h], p, i, True).wait_recv()

        def box(h, p, i, upward):
            d = flip if upward else 1 - flip
            where = came.at[d, sides[h], place(p), i]
            back(where, sides[h], p, i, upward).wait_recv()
            return where

        for kind, h, p, i, way in ops:
            s = place(p)
            if kind == SEND:
                need(h, p, i)
                push(sides[h], p, i, way > 0).start()
            elif kind == WORK:
                blocks = (0, 1) if i == 2 else (i,)
                for block in blocks:
                    need(h, p, block)
                if not weights:
                    weights.append(1)
                    for copy in (own_in, own_out, mate_in, mate_out):
                        copy.wait()
                work(s, blocks[0], len(blocks))
            elif kind == ADD:
                if role == 0:
                    ways = [False]
                elif p == 1:
                    ways = [False, True]
                else:
                    ways = [p in (2, 3, 4, 5)]
                add(s, i, [box(h, p, i, w) for w in ways])
            elif kind == BACK:
                src = box(h, p, i, True) if h == 1 else part.at[s, i]
                back(src, sides[h], p, i, way > 0).start()
            else:
                src = box(h, p, i, True) if h == 1 else part.at[s, i]
                deliver(src, sides[h], i).start()
        for kind, h, p, i, way in ops:
            if kind == SEND:
                push(sides[h], p, i, way > 0).wait_send()
            elif kind == BACK:
                back(part.at[0, 0], sides[h], p, i, way > 0).wait_send()
            elif kind == LAST:
                deliver(part.at[0, 0], sides[h], i).wait_send()

    own_in.start()
    own_out.start()
    gather(2 * (1 - x) + own, cross.at[own])
    gather(2 * x + own, rows.at[own, y, 0])
    gather(2 * x + far, rows.at[far, y, 0])
    gather(2 * (1 - x) + far, cross.at[far])
    pl.semaphore_wait(barrier, len(partners))
    for h in (own, far):
        crossing(h).start()
    mate_in.start()
    mate_out.start()
    for j in range(4):
        taken, amount = slots(j)
        table_out[j] = (taken * amount).astype(BF)
    table = remote(table_out, table_in, table_send, table_recv, (after, me))

    @pl.when(edge)
    def _():
        run(0, EDGE)

    @pl.when(inner)
    def _():
        run(1, INNER)

    keep.wait()
    table.wait()
    for j in range(4):
        remote(
            result.at[j], result.at[j], last_send.at[0, 0], last_recv.at[j], (after, me)
        ).wait_recv()

    @pl.loop(0, chunks)
    def _(k):
        cols = pl.ds(pl.multiple_of(k * WIDE, WIDE), WIDE)
        total = resid[:, cols].astype(F32)
        for j in range(4):
            total += lax.dot_general(
                table_in[j], result[j, :, cols], (((0,), (0,)), ((), ())),
                preferred_element_type=F32,
            )
        out[:, cols] = total.astype(BF)

    for h in range(2):
        crossing(h).wait_send()


def local(acts, expert_ids, gate_weights, norm_gain, w_in, w_out):
    tok, width = acts.shape[1:]
    hid = w_out.shape[1]
    vmem = pl.BlockSpec(memory_space=pltpu.VMEM)
    hbm = pl.BlockSpec(memory_space=pl.ANY)
    dma = pltpu.SemaphoreType.DMA
    flat_in = w_in[0].transpose(1, 0, 2).reshape(2 * hid, width)
    moved = pl.pallas_call(
        relay,
        out_shape=jax.ShapeDtypeStruct((tok, width), BF),
        in_specs=[vmem, vmem, vmem, vmem, hbm, hbm],
        out_specs=vmem,
        scratch_shapes=[
            pltpu.VMEM((2, 2 * hid, width), BF),
            pltpu.VMEM((2, hid, width), BF),
            pltpu.VMEM((tok, width), BF),
            pltpu.VMEM((4, CAP, tok), BF),
            pltpu.VMEM((4, CAP, tok), BF),
            pltpu.VMEM((tok, width), BF),
            pltpu.VMEM((2, RING, 2, CAP, width), BF),
            pltpu.VMEM((2, CAP, width), BF),
            pltpu.VMEM((RING, 2, CAP, width), BF),
            pltpu.VMEM((2, 2, RING, 2, CAP, width), BF),
            pltpu.VMEM((4, CAP, width), BF),
            dma((2,)), dma((2,)), dma((2,)), dma, dma, dma, dma,
            dma((2,)), dma((2,)), dma((2, 2, RING, 2)), dma((2, RING, 2)),
            dma((2, RING, 2)), dma((2, 2, RING, 2)), dma((2, 2)), dma((4,)),
        ],
        compiler_params=pltpu.CompilerParams(
            collective_id=0, has_side_effects=True, vmem_limit_bytes=60 * 2**20
        ),
    )(acts[0], expert_ids[0].T, gate_weights[0].T, norm_gain, flat_in, w_out[0])
    return moved[None]


def solution(mesh):
    placed = (
        P("section", "expert", None),
        P("section", "expert", None),
        P("section", "expert", None),
        P("section", None),
        P("section", "expert", None, None),
        P("section", "expert", None),
    )
    return jax.shard_map(
        local, mesh=mesh, in_specs=placed, out_specs=P("section", "expert", None), check_vma=False
    )
```

```python
import jax
import jax.numpy as jnp
from jax import lax
from jax.experimental import pallas as pl
from jax.experimental.pallas import tpu as pltpu
from jax.sharding import PartitionSpec as P

CAP = 24
RING = 8
HALF = 4
WIDE = 512
HUGE = 1792
MESH = pl.DeviceIdType.MESH
BF = jnp.bfloat16
F32 = jnp.float32
SEND, WORK, ADD, BACK, LAST = range(5)
EDGE = (
    (0, 0, 0, 0, 1), (0, 1, 0, 0, -1), (0, 1, 1, 0, -1), (0, 0, 7, 0, 1), (1, 0, 0, 0, 0),
    (0, 0, 0, 1, 1), (1, 0, 7, 0, 0), (1, 0, 1, 0, 0), (0, 1, 0, 1, -1), (0, 0, 6, 0, 1),
    (1, 0, 6, 0, 0), (1, 0, 2, 0, 0), (0, 0, 7, 1, 1), (1, 0, 7, 1, 0), (0, 1, 1, 1, -1),
    (3, 0, 1, 0, 1), (1, 0, 0, 1, 0), (1, 0, 2, 1, 0), (0, 0, 6, 1, 1), (1, 0, 6, 1, 0),
    (3, 0, 2, 1, 1), (1, 0, 3, 0, 0), (1, 0, 4, 0, 0), (3, 0, 4, 0, 1), (1, 0, 5, 0, 0),
    (3, 0, 5, 0, 1), (1, 0, 1, 1, 0), (3, 0, 1, 1, 1), (1, 0, 3, 1, 0), (3, 0, 3, 1, 1),
    (1, 0, 5, 1, 0), (3, 0, 5, 1, 1), (1, 0, 4, 1, 0), (3, 0, 4, 1, 1), (3, 0, 3, 0, 1),
    (2, 0, 7, 0, 1), (3, 0, 7, 0, -1), (3, 0, 2, 0, 1), (2, 0, 6, 0, 1), (3, 0, 6, 0, -1),
    (4, 1, 0, 0, 0), (2, 0, 0, 1, 1), (4, 0, 0, 1, 0), (3, 1, 1, 0, 1), (2, 0, 6, 1, 1),
    (3, 0, 6, 1, -1), (2, 0, 7, 1, 1), (3, 0, 7, 1, -1), (3, 1, 1, 1, 1), (2, 0, 0, 0, 1),
    (4, 0, 0, 0, 0), (4, 1, 0, 1, 0),
)
INNER = (
    (0, 0, 1, 0, 1), (0, 1, 1, 0, -1), (0, 0, 1, 0, -1), (0, 0, 0, 0, 1), (0, 0, 2, 0, -1),
    (1, 0, 1, 0, 0), (0, 0, 1, 1, 1), (1, 0, 0, 0, 0), (1, 0, 1, 1, 0), (0, 1, 1, 1, -1),
    (0, 0, 7, 0, 1), (1, 0, 7, 0, 0), (1, 0, 2, 0, 0), (0, 0, 2, 1, -1), (0, 0, 0, 1, 1),
    (1, 0, 0, 1, 0), (0, 0, 3, 0, -1), (1, 0, 2, 1, 0), (0, 0, 6, 0, 1), (0, 0, 4, 0, -1),
    (1, 0, 6, 0, 0), (1, 0, 4, 0, 0), (0, 0, 7, 1, 1), (1, 0, 7, 1, 0), (1, 0, 3, 2, 0),
    (0, 0, 5, 0, -1), (0, 0, 1, 1, -1), (1, 0, 5, 0, 0), (0, 0, 6, 1, 1), (1, 0, 6, 1, 0),
    (0, 0, 3, 1, -1), (1, 0, 4, 1, 0), (2, 0, 2, 1, 1), (3, 0, 2, 1, 1), (0, 0, 5, 1, -1),
    (1, 0, 5, 1, 0), (2, 0, 4, 0, 1), (3, 0, 4, 0, 1), (0, 0, 4, 1, -1), (2, 0, 5, 0, 1),
    (3, 0, 5, 0, 1), (2, 0, 7, 0, 1), (3, 0, 7, 0, -1), (2, 0, 1, 1, 2), (4, 0, 1, 1, 0),
    (2, 0, 6, 0, 1), (3, 0, 6, 0, -1), (2, 0, 3, 1, 1), (3, 0, 3, 1, 1), (2, 0, 5, 1, 1),
    (3, 0, 5, 1, 1), (2, 0, 0, 1, 1), (3, 0, 0, 1, -1), (2, 0, 4, 1, 1), (3, 0, 4, 1, 1),
    (2, 0, 6, 1, 1), (3, 0, 6, 1, -1), (2, 0, 3, 0, 1), (3, 0, 3, 0, 1), (2, 0, 7, 1, 1),
    (3, 0, 7, 1, -1), (2, 0, 2, 0, 1), (3, 0, 2, 0, 1), (2, 0, 0, 0, 1), (3, 0, 0, 0, -1),
    (4, 1, 1, 0, 0), (2, 0, 1, 0, 2), (4, 0, 1, 0, 0), (4, 1, 1, 1, 0),
)


def relay(
    acts, ids, gates, gain, w_in, w_out,
    resid, table_in, result,
    win, wout, table_out, normed,
    rows, cross, part, came,
    local_sem, w_send, w_recv, acts_send, acts_recv, table_send, table_recv,
    cross_send, cross_recv, out_send, out_recv,
    back_send, back_recv, last_send, last_recv,
):
    tok, width = acts.shape
    chunks = width // WIDE
    sec = lax.axis_index("section")
    me = lax.axis_index("expert")
    n_sec = lax.axis_size("section")
    x, y, core = me // 16, (me // 2) % RING, me % 2
    own = y // HALF
    r = y % HALF
    flip = (r >= 2).astype(jnp.int32)
    edge = jnp.logical_or(r == 0, r == 3)
    inner = jnp.logical_not(edge)
    up = 1 - 2 * flip
    far = 1 - own

    def at(col, row, c):
        return col * 16 + row * 2 + c

    def ring(step):
        return at(x, (y + step + RING) % RING, core)

    up_dev, down_dev = ring(up), ring(-up)
    across = at(1 - x, y, core)
    mate = at(x, y, 1 - core)
    after, before = (sec + 1) % n_sec, (sec + n_sec - 1) % n_sec

    def place(p):
        return (own * HALF + 3 * flip + up * p + 2 * RING) % RING

    barrier = pltpu.get_barrier_semaphore()
    partners = [
        (sec, up_dev), (sec, down_dev), (sec, across), (sec, mate),
        (after, me), (after, across), (before, me), (before, across),
    ]
    for who in partners:
        pl.semaphore_signal(barrier, inc=1, device_id=who, device_id_type=MESH)

    def remote(src, dst, send, recv, who):
        return pltpu.make_async_remote_copy(
            src_ref=src, dst_ref=dst, send_sem=send, recv_sem=recv,
            device_id=who, device_id_type=MESH,
        )

    own_in = pltpu.make_async_copy(w_in, win.at[core], local_sem.at[0])
    own_out = pltpu.make_async_copy(w_out, wout.at[core], local_sem.at[1])
    mate_in = remote(w_in, win.at[core], w_send.at[0], w_recv.at[0], (sec, mate))
    mate_out = remote(w_out, wout.at[core], w_send.at[1], w_recv.at[1], (sec, mate))
    keep = remote(acts, resid, acts_send, acts_recv, (after, me))

    blocks = (2 * (1 - x) + own, 2 * x + own, 2 * x + far, 2 * (1 - x) + far)
    chosen = ids[...]
    weight = gates[...].astype(F32)
    line = lax.broadcasted_iota(jnp.int32, (4 * CAP, tok), 0)
    wanted, index = jnp.zeros_like(line), line
    for k, j in enumerate(blocks):
        inside = jnp.logical_and(line >= k * CAP, line < (k + 1) * CAP)
        wanted = jnp.where(inside, j, wanted)
        index = jnp.where(inside, line - k * CAP, index)
    present = jnp.zeros((4 * CAP, tok), F32)
    amount = jnp.zeros((4 * CAP, tok), F32)
    for k in range(ids.shape[0]):
        hit = chosen[k:k + 1] == wanted
        present = jnp.where(hit, 1.0, present)
        amount = jnp.where(hit, weight[k:k + 1], amount)
    earlier = (
        lax.broadcasted_iota(jnp.int32, (tok, tok), 0)
        < lax.broadcasted_iota(jnp.int32, (tok, tok), 1)
    ).astype(BF)
    count = jnp.dot(present.astype(BF), earlier, preferred_element_type=F32)
    taken = jnp.where(index.astype(F32) == count, present, 0.0)
    pick = taken.astype(BF)
    table_out[...] = (taken * amount).astype(BF)

    @pl.loop(0, tok // 16)
    def _(i):
        block = pl.ds(pl.multiple_of(i * 16, 16), 16)
        v = acts[block, :].astype(F32)
        mean = jnp.mean(v * v, axis=-1, keepdims=True)
        normed[block, :] = (v * lax.rsqrt(mean + 1e-06) * gain[...]).astype(BF)

    @pl.loop(0, chunks)
    def _(k):
        cols = pl.ds(pl.multiple_of(k * WIDE, WIDE), WIDE)
        packed = jnp.dot(pick, normed[:, cols], preferred_element_type=F32)
        places = (cross.at[own], rows.at[own, y, 0], rows.at[far, y, 0], cross.at[far])
        for b, dst in enumerate(places):
            dst[:, cols] = packed[b * CAP:(b + 1) * CAP].astype(BF)

    def push(h, p, i, upward):
        s = place(p)
        d = flip if upward else 1 - flip
        return remote(
            rows.at[h, s, i], rows.at[h, s, i], out_send.at[d, h, s, i],
            out_recv.at[h, s, i], (sec, up_dev if upward else down_dev),
        )

    def back(src, h, p, i, upward):
        s = place(p)
        d = flip if upward else 1 - flip
        return remote(
            src, came.at[d, h, s, i], back_send.at[h, s, i], back_recv.at[d, h, s, i],
            (sec, up_dev if upward else down_dev),
        )

    def crossing(h):
        return remote(
            cross.at[h], rows.at[h, y, 1], cross_send.at[h], cross_recv.at[h], (sec, across)
        )

    def deliver(src, side, i):
        b = ((1, 0), (2, 3))[side][i]
        return remote(
            src, result.at[b], last_send.at[b], last_recv.at[b],
            (after, me if i == 0 else across),
        )

    def work(s, first, count):
        def step(k, acc):
            cols = pl.ds(pl.multiple_of(k * HUGE, HUGE), HUGE)
            block = rows[own, s, first:first + count, :, cols].reshape(count * CAP, HUGE)
            return tuple(
                acc[c] + lax.dot_general(
                    block, win[c, :, cols], (((1,), (1,)), ((), ())),
                    preferred_element_type=F32,
                )
                for c in range(2)
            )

        zero = jnp.zeros((count * CAP, 256), F32)
        both = lax.fori_loop(0, width // HUGE, step, (zero, zero))
        hid = jnp.concatenate(
            [(jax.nn.silu(v[:, :128]) * v[:, 128:]).astype(BF) for v in both], axis=1
        )

        @pl.loop(0, width // HUGE)
        def _(k):
            cols = pl.ds(pl.multiple_of(k * HUGE, HUGE), HUGE)
            part[s, first:first + count, :, cols] = jnp.dot(
                hid, wout[:, :, cols].reshape(256, HUGE), preferred_element_type=F32
            ).astype(BF).reshape(count, CAP, HUGE)

    def add(s, i, boxes):
        @pl.loop(0, chunks)
        def _(k):
            cols = pl.ds(pl.multiple_of(k * WIDE, WIDE), WIDE)
            total = part[s, i, :, cols].astype(F32)
            for box in boxes:
                total += box[:, cols].astype(F32)
            part[s, i, :, cols] = total.astype(BF)

    sides = (own, far)

    def run(role, ops):
        seen, weights = {(h, role, 0) for h in range(2)}, []

        def need(h, p, i):
            if (h, p, i) in seen:
                return
            seen.add((h, p, i))
            if p == role:
                crossing(sides[h]).wait_recv()
                if {(0, role, 1), (1, role, 1)} <= seen:
                    keep.start()
                    table.start()
            else:
                push(sides[h], p, i, True).wait_recv()

        def box(h, p, i, upward):
            d = flip if upward else 1 - flip
            where = came.at[d, sides[h], place(p), i]
            back(where, sides[h], p, i, upward).wait_recv()
            return where

        for kind, h, p, i, way in ops:
            s = place(p)
            if kind == SEND:
                need(h, p, i)
                push(sides[h], p, i, way > 0).start()
            elif kind == WORK:
                blocks = (0, 1) if i == 2 else (i,)
                for block in blocks:
                    need(h, p, block)
                if not weights:
                    weights.append(1)
                    for copy in (own_in, own_out, mate_in, mate_out):
                        copy.wait()
                work(s, blocks[0], len(blocks))
            elif kind == ADD:
                if role == 0:
                    ways = [False]
                elif p == 1:
                    ways = [False, True]
                else:
                    ways = [p in (2, 3, 4, 5)]
                add(s, i, [box(h, p, i, w) for w in ways])
            elif kind == BACK:
                src = box(h, p, i, True) if h == 1 else part.at[s, i]
                back(src, sides[h], p, i, way > 0).start()
            else:
                src = box(h, p, i, True) if h == 1 else part.at[s, i]
                deliver(src, h, i).start()
        for kind, h, p, i, way in ops:
            if kind == SEND:
                push(sides[h], p, i, way > 0).wait_send()
            elif kind == BACK:
                back(part.at[0, 0], sides[h], p, i, way > 0).wait_send()
            elif kind == LAST:
                deliver(part.at[0, 0], h, i).wait_send()

    own_in.start()
    own_out.start()
    pl.semaphore_wait(barrier, len(partners))
    for h in (own, far):
        crossing(h).start()
    mate_in.start()
    mate_out.start()
    table = remote(table_out, table_in, table_send, table_recv, (after, me))

    @pl.when(edge)
    def _():
        run(0, EDGE)

    @pl.when(inner)
    def _():
        run(1, INNER)

    keep.wait()
    table.wait()
    for b in range(4):
        remote(
            result.at[b], result.at[b], last_send.at[b], last_recv.at[b], (after, me)
        ).wait_recv()
    for h in range(2):
        crossing(h).wait_send()


def local(acts, expert_ids, gate_weights, norm_gain, w_in, w_out):
    tok, width = acts.shape[1:]
    hid = w_out.shape[1]
    vmem = pl.BlockSpec(memory_space=pltpu.VMEM)
    hbm = pl.BlockSpec(memory_space=pl.ANY)
    dma = pltpu.SemaphoreType.DMA
    flat_in = w_in[0].transpose(1, 0, 2).reshape(2 * hid, width)
    resid, table, result = pl.pallas_call(
        relay,
        out_shape=(
            jax.ShapeDtypeStruct((tok, width), BF),
            jax.ShapeDtypeStruct((4 * CAP, tok), BF),
            jax.ShapeDtypeStruct((4, CAP, width), BF),
        ),
        in_specs=[vmem, vmem, vmem, vmem, hbm, hbm],
        out_specs=(hbm, hbm, hbm),
        scratch_shapes=[
            pltpu.VMEM((2, 2 * hid, width), BF),
            pltpu.VMEM((2, hid, width), BF),
            pltpu.VMEM((4 * CAP, tok), BF),
            pltpu.VMEM((tok, width), BF),
            pltpu.VMEM((2, RING, 2, CAP, width), BF),
            pltpu.VMEM((2, CAP, width), BF),
            pltpu.VMEM((RING, 2, CAP, width), BF),
            pltpu.VMEM((2, 2, RING, 2, CAP, width), BF),
            dma((2,)), dma((2,)), dma((2,)), dma, dma, dma, dma,
            dma((2,)), dma((2,)), dma((2, 2, RING, 2)), dma((2, RING, 2)),
            dma((2, RING, 2)), dma((2, 2, RING, 2)), dma((4,)), dma((4,)),
        ],
        compiler_params=pltpu.CompilerParams(
            collective_id=0, has_side_effects=True, vmem_limit_bytes=60 * 2**20
        ),
    )(acts[0], expert_ids[0].T, gate_weights[0].T, norm_gain, flat_in, w_out[0])
    delta = lax.dot_general(
        table, result.reshape(4 * CAP, width), (((0,), (0,)), ((), ())),
        preferred_element_type=F32,
    )
    return (resid.astype(F32) + delta).astype(BF)[None]


def solution(mesh):
    placed = (
        P("section", "expert", None),
        P("section", "expert", None),
        P("section", "expert", None),
        P("section", None),
        P("section", "expert", None, None),
        P("section", "expert", None),
    )
    return jax.shard_map(
        local, mesh=mesh, in_specs=placed, out_specs=P("section", "expert", None), check_vma=False
    )
```

```python
import jax
import jax.numpy as jnp
from jax import lax
from jax.experimental import pallas as pl
from jax.experimental.pallas import tpu as pltpu
from jax.sharding import PartitionSpec as P

CAP = 24
RING = 8
HALF = 4
WIDE = 512
HUGE = 1792
THIN = 896
ENDING = {(0, 0, 1, 1), (0, 0, 7, -1), (0, 1, 1, 1), (1, 0, 0, -1), (1, 0, 2, 1)}
MESH = pl.DeviceIdType.MESH
BF = jnp.bfloat16
F32 = jnp.float32
SEND, WORK, ADD, BACK, LAST = range(5)
EDGE = (
    (0, 0, 0, 0, 1), (0, 1, 0, 0, -1), (0, 1, 1, 0, -1), (0, 0, 7, 0, 1), (1, 0, 0, 0, 0),
    (0, 0, 0, 1, 1), (1, 0, 7, 0, 0), (1, 0, 1, 0, 0), (0, 1, 0, 1, -1), (0, 0, 6, 0, 1),
    (1, 0, 6, 0, 0), (1, 0, 2, 0, 0), (0, 0, 7, 1, 1), (1, 0, 7, 1, 0), (0, 1, 1, 1, -1),
    (3, 0, 1, 0, 1), (1, 0, 0, 1, 0), (1, 0, 2, 1, 0), (0, 0, 6, 1, 1), (1, 0, 6, 1, 0),
    (3, 0, 2, 1, 1), (1, 0, 3, 0, 0), (1, 0, 4, 0, 0), (3, 0, 4, 0, 1), (1, 0, 5, 0, 0),
    (3, 0, 5, 0, 1), (1, 0, 1, 1, 0), (3, 0, 1, 1, 1), (1, 0, 3, 1, 0), (3, 0, 3, 1, 1),
    (1, 0, 5, 1, 0), (3, 0, 5, 1, 1), (1, 0, 4, 1, 0), (3, 0, 4, 1, 1), (3, 0, 3, 0, 1),
    (2, 0, 7, 0, 1), (3, 0, 7, 0, -1), (3, 0, 2, 0, 1), (2, 0, 6, 0, 1), (3, 0, 6, 0, -1),
    (4, 1, 0, 0, 0), (2, 0, 0, 1, 1), (4, 0, 0, 1, 0), (3, 1, 1, 0, 1), (2, 0, 6, 1, 1),
    (3, 0, 6, 1, -1), (2, 0, 7, 1, 1), (3, 0, 7, 1, -1), (3, 1, 1, 1, 1), (2, 0, 0, 0, 1),
    (4, 0, 0, 0, 0), (4, 1, 0, 1, 0),
)
INNER = (
    (0, 0, 1, 0, 1), (0, 1, 1, 0, -1), (0, 0, 1, 0, -1), (0, 0, 0, 0, 1), (0, 0, 2, 0, -1),
    (1, 0, 1, 0, 0), (0, 0, 1, 1, 1), (1, 0, 0, 0, 0), (1, 0, 1, 1, 0), (0, 1, 1, 1, -1),
    (0, 0, 7, 0, 1), (1, 0, 7, 0, 0), (1, 0, 2, 0, 0), (0, 0, 2, 1, -1), (0, 0, 0, 1, 1),
    (1, 0, 0, 1, 0), (0, 0, 3, 0, -1), (1, 0, 2, 1, 0), (0, 0, 6, 0, 1), (0, 0, 4, 0, -1),
    (1, 0, 6, 0, 0), (1, 0, 4, 0, 0), (0, 0, 7, 1, 1), (1, 0, 7, 1, 0), (1, 0, 3, 2, 0),
    (0, 0, 5, 0, -1), (0, 0, 1, 1, -1), (1, 0, 5, 0, 0), (0, 0, 6, 1, 1), (1, 0, 6, 1, 0),
    (0, 0, 3, 1, -1), (1, 0, 4, 1, 0), (2, 0, 2, 1, 1), (3, 0, 2, 1, 1), (0, 0, 5, 1, -1),
    (1, 0, 5, 1, 0), (2, 0, 4, 0, 1), (3, 0, 4, 0, 1), (0, 0, 4, 1, -1), (2, 0, 5, 0, 1),
    (3, 0, 5, 0, 1), (2, 0, 7, 0, 1), (3, 0, 7, 0, -1), (2, 0, 1, 1, 2), (4, 0, 1, 1, 0),
    (2, 0, 6, 0, 1), (3, 0, 6, 0, -1), (2, 0, 3, 1, 1), (3, 0, 3, 1, 1), (2, 0, 5, 1, 1),
    (3, 0, 5, 1, 1), (2, 0, 0, 1, 1), (3, 0, 0, 1, -1), (2, 0, 4, 1, 1), (3, 0, 4, 1, 1),
    (2, 0, 6, 1, 1), (3, 0, 6, 1, -1), (2, 0, 3, 0, 1), (3, 0, 3, 0, 1), (2, 0, 7, 1, 1),
    (3, 0, 7, 1, -1), (2, 0, 2, 0, 1), (3, 0, 2, 0, 1), (2, 0, 0, 0, 1), (3, 0, 0, 0, -1),
    (4, 1, 1, 0, 0), (2, 0, 1, 0, 2), (4, 0, 1, 0, 0), (4, 1, 1, 1, 0),
)


def relay(
    acts, ids, gates, gain, w_in, w_out,
    resid, table_in, result,
    win, wout, table_out, normed,
    rows, cross, part, came,
    local_sem, w_send, w_recv, acts_send, acts_recv, table_send, table_recv,
    cross_send, cross_recv, out_send, out_recv,
    back_send, back_recv, last_send, last_recv,
):
    tok, width = acts.shape
    chunks = width // WIDE
    sec = lax.axis_index("section")
    me = lax.axis_index("expert")
    n_sec = lax.axis_size("section")
    x, y, core = me // 16, (me // 2) % RING, me % 2
    own = y // HALF
    r = y % HALF
    flip = (r >= 2).astype(jnp.int32)
    edge = jnp.logical_or(r == 0, r == 3)
    inner = jnp.logical_not(edge)
    up = 1 - 2 * flip
    far = 1 - own

    def at(col, row, c):
        return col * 16 + row * 2 + c

    def ring(step):
        return at(x, (y + step + RING) % RING, core)

    up_dev, down_dev = ring(up), ring(-up)
    across = at(1 - x, y, core)
    mate = at(x, y, 1 - core)
    after, before = (sec + 1) % n_sec, (sec + n_sec - 1) % n_sec

    def place(p):
        return (own * HALF + 3 * flip + up * p + 2 * RING) % RING

    barrier = pltpu.get_barrier_semaphore()
    partners = [
        (sec, up_dev), (sec, down_dev), (sec, across), (sec, mate),
        (after, me), (after, across), (before, me), (before, across),
    ]
    for who in partners:
        pl.semaphore_signal(barrier, inc=1, device_id=who, device_id_type=MESH)

    def remote(src, dst, send, recv, who):
        return pltpu.make_async_remote_copy(
            src_ref=src, dst_ref=dst, send_sem=send, recv_sem=recv,
            device_id=who, device_id_type=MESH,
        )

    own_in = pltpu.make_async_copy(w_in, win.at[core], local_sem.at[0])
    own_out = pltpu.make_async_copy(w_out, wout.at[core], local_sem.at[1])
    mate_in = remote(w_in, win.at[core], w_send.at[0], w_recv.at[0], (sec, mate))
    mate_out = remote(w_out, wout.at[core], w_send.at[1], w_recv.at[1], (sec, mate))
    keep = remote(acts, resid, acts_send, acts_recv, (after, me))

    blocks = (2 * (1 - x) + own, 2 * x + own, 2 * x + far, 2 * (1 - x) + far)
    chosen = ids[...]
    weight = gates[...].astype(F32)
    line = lax.broadcasted_iota(jnp.int32, (4 * CAP, tok), 0)
    wanted, index = jnp.zeros_like(line), line
    for k, j in enumerate(blocks):
        inside = jnp.logical_and(line >= k * CAP, line < (k + 1) * CAP)
        wanted = jnp.where(inside, j, wanted)
        index = jnp.where(inside, line - k * CAP, index)
    present = jnp.zeros((4 * CAP, tok), F32)
    amount = jnp.zeros((4 * CAP, tok), F32)
    for k in range(ids.shape[0]):
        hit = chosen[k:k + 1] == wanted
        present = jnp.where(hit, 1.0, present)
        amount = jnp.where(hit, weight[k:k + 1], amount)
    earlier = (
        lax.broadcasted_iota(jnp.int32, (tok, tok), 0)
        < lax.broadcasted_iota(jnp.int32, (tok, tok), 1)
    ).astype(BF)
    count = jnp.dot(present.astype(BF), earlier, preferred_element_type=F32)
    taken = jnp.where(index.astype(F32) == count, present, 0.0)
    pick = taken.astype(BF)
    table_out[...] = (taken * amount).astype(BF)

    @pl.loop(0, tok // 16)
    def _(i):
        block = pl.ds(pl.multiple_of(i * 16, 16), 16)
        v = acts[block, :].astype(F32)
        mean = jnp.mean(v * v, axis=-1, keepdims=True)
        normed[block, :] = (v * lax.rsqrt(mean + 1e-06) * gain[...]).astype(BF)

    @pl.loop(0, chunks)
    def _(k):
        cols = pl.ds(pl.multiple_of(k * WIDE, WIDE), WIDE)
        packed = jnp.dot(pick, normed[:, cols], preferred_element_type=F32)
        places = (cross.at[own], rows.at[own, y, 0], rows.at[far, y, 0], cross.at[far])
        for b, dst in enumerate(places):
            dst[:, cols] = packed[b * CAP:(b + 1) * CAP].astype(BF)

    def push(h, p, i, upward):
        s = place(p)
        d = flip if upward else 1 - flip
        return remote(
            rows.at[h, s, i], rows.at[h, s, i], out_send.at[d, h, s, i],
            out_recv.at[h, s, i], (sec, up_dev if upward else down_dev),
        )

    def back(src, h, p, i, upward, k, cols):
        s = place(p)
        d = flip if upward else 1 - flip
        return remote(
            src.at[:, cols], came.at[d, h, s, i, :, cols],
            back_send.at[h, s, i, k], back_recv.at[d, h, s, i, k],
            (sec, up_dev if upward else down_dev),
        )

    whole = (pl.ds(0, width),)
    halves = (pl.ds(0, width // 2), pl.ds(width // 2, width // 2))

    def crossing(h):
        return remote(
            cross.at[h], rows.at[h, y, 1], cross_send.at[h], cross_recv.at[h], (sec, across)
        )

    def deliver(src, side, i, k):
        b = ((1, 0), (2, 3))[side][i]
        return remote(
            src.at[:, halves[k]], result.at[b, :, halves[k]],
            last_send.at[b, k], last_recv.at[b, k],
            (after, me if i == 0 else across),
        )

    def work(s, first, count):
        def step(k, acc):
            cols = pl.ds(pl.multiple_of(k * HUGE, HUGE), HUGE)
            block = rows[own, s, first:first + count, :, cols].reshape(count * CAP, HUGE)
            return tuple(
                acc[c] + lax.dot_general(
                    block, win[c, :, cols], (((1,), (1,)), ((), ())),
                    preferred_element_type=F32,
                )
                for c in range(2)
            )

        zero = jnp.zeros((count * CAP, 256), F32)
        both = lax.fori_loop(0, width // HUGE, step, (zero, zero))
        hid = jnp.concatenate(
            [(jax.nn.silu(v[:, :128]) * v[:, 128:]).astype(BF) for v in both], axis=1
        )

        @pl.loop(0, width // HUGE)
        def _(k):
            cols = pl.ds(pl.multiple_of(k * HUGE, HUGE), HUGE)
            part[s, first:first + count, :, cols] = jnp.dot(
                hid, wout[:, :, cols].reshape(256, HUGE), preferred_element_type=F32
            ).astype(BF).reshape(count, CAP, HUGE)

    def add(s, i, boxes, begin, count):
        @pl.loop(0, count // THIN)
        def _(k):
            cols = pl.ds(pl.multiple_of(begin + k * THIN, 128), THIN)
            total = part[s, i, :, cols].astype(F32)
            for box in boxes:
                total += box[:, cols].astype(F32)
            part[s, i, :, cols] = total.astype(BF)

    sides = (own, far)

    def run(role, ops):
        seen, weights = {(h, role, 0) for h in range(2)}, []

        def need(h, p, i):
            if (h, p, i) in seen:
                return
            seen.add((h, p, i))
            if p == role:
                crossing(sides[h]).wait_recv()
                if {(0, role, 1), (1, role, 1)} <= seen:
                    keep.start()
                    table.start()
            else:
                push(sides[h], p, i, True).wait_recv()

        def box(h, p, i, upward, k=None):
            d = flip if upward else 1 - flip
            where = came.at[d, sides[h], place(p), i]
            cols = whole[0] if k is None else halves[k]
            back(where, sides[h], p, i, upward, k or 0, cols).wait_recv()
            return where

        def cuts(h, p, way):
            return halves if (role, h, p, way) in ENDING else whole

        for kind, h, p, i, way in ops:
            s = place(p)
            if kind == SEND:
                need(h, p, i)
                push(sides[h], p, i, way > 0).start()
            elif kind == WORK:
                blocks = (0, 1) if i == 2 else (i,)
                for block in blocks:
                    need(h, p, block)
                if not weights:
                    weights.append(1)
                    for copy in (own_in, own_out, mate_in, mate_out):
                        copy.wait()
                work(s, blocks[0], len(blocks))
            elif kind == ADD:
                if role == 0:
                    ways = [False]
                elif p == 1:
                    ways = [False, True]
                else:
                    ways = [p in (2, 3, 4, 5)]
                if p == role:
                    for k in range(2):
                        boxes = [box(h, p, i, w, k) for w in ways]
                        add(s, i, boxes, k * (width // 2), width // 2)
                        deliver(part.at[s, i], h, i, k).start()
                else:
                    add(s, i, [box(h, p, i, w) for w in ways], 0, width)
            elif kind == BACK:
                src = box(h, p, i, True) if h == 1 else part.at[s, i]
                for k, cols in enumerate(cuts(h, p, way)):
                    back(src, sides[h], p, i, way > 0, k, cols).start()
            elif h == 1:
                for k in range(2):
                    deliver(box(h, p, i, True, k), h, i, k).start()
        for kind, h, p, i, way in ops:
            if kind == SEND:
                push(sides[h], p, i, way > 0).wait_send()
            elif kind == BACK:
                for k, cols in enumerate(cuts(h, p, way)):
                    back(part.at[0, 0], sides[h], p, i, way > 0, k, cols).wait_send()
            elif kind == LAST:
                for k in range(2):
                    deliver(part.at[0, 0], h, i, k).wait_send()

    own_in.start()
    own_out.start()
    pl.semaphore_wait(barrier, len(partners))
    for h in (own, far):
        crossing(h).start()
    mate_in.start()
    mate_out.start()
    table = remote(table_out, table_in, table_send, table_recv, (after, me))

    @pl.when(edge)
    def _():
        run(0, EDGE)

    @pl.when(inner)
    def _():
        run(1, INNER)

    keep.wait()
    table.wait()
    for b in range(4):
        for k, cols in enumerate(halves):
            remote(
                result.at[b, :, cols], result.at[b, :, cols],
                last_send.at[b, k], last_recv.at[b, k], (after, me),
            ).wait_recv()
    for h in range(2):
        crossing(h).wait_send()


def local(acts, expert_ids, gate_weights, norm_gain, w_in, w_out):
    tok, width = acts.shape[1:]
    hid = w_out.shape[1]
    vmem = pl.BlockSpec(memory_space=pltpu.VMEM)
    hbm = pl.BlockSpec(memory_space=pl.ANY)
    dma = pltpu.SemaphoreType.DMA
    flat_in = w_in[0].transpose(1, 0, 2).reshape(2 * hid, width)
    resid, table, result = pl.pallas_call(
        relay,
        out_shape=(
            jax.ShapeDtypeStruct((tok, width), BF),
            jax.ShapeDtypeStruct((4 * CAP, tok), BF),
            jax.ShapeDtypeStruct((4, CAP, width), BF),
        ),
        in_specs=[vmem, vmem, vmem, vmem, hbm, hbm],
        out_specs=(hbm, hbm, hbm),
        scratch_shapes=[
            pltpu.VMEM((2, 2 * hid, width), BF),
            pltpu.VMEM((2, hid, width), BF),
            pltpu.VMEM((4 * CAP, tok), BF),
            pltpu.VMEM((tok, width), BF),
            pltpu.VMEM((2, RING, 2, CAP, width), BF),
            pltpu.VMEM((2, CAP, width), BF),
            pltpu.VMEM((RING, 2, CAP, width), BF),
            pltpu.VMEM((2, 2, RING, 2, CAP, width), BF),
            dma((2,)), dma((2,)), dma((2,)), dma, dma, dma, dma,
            dma((2,)), dma((2,)), dma((2, 2, RING, 2)), dma((2, RING, 2)),
            dma((2, RING, 2, 2)), dma((2, 2, RING, 2, 2)), dma((4, 2)), dma((4, 2)),
        ],
        compiler_params=pltpu.CompilerParams(
            collective_id=0, has_side_effects=True, vmem_limit_bytes=60 * 2**20
        ),
    )(acts[0], expert_ids[0].T, gate_weights[0].T, norm_gain, flat_in, w_out[0])
    delta = lax.dot_general(
        table, result.reshape(4 * CAP, width), (((0,), (0,)), ((), ())),
        preferred_element_type=F32,
    )
    return (resid.astype(F32) + delta).astype(BF)[None]


def solution(mesh):
    placed = (
        P("section", "expert", None),
        P("section", "expert", None),
        P("section", "expert", None),
        P("section", None),
        P("section", "expert", None, None),
        P("section", "expert", None),
    )
    return jax.shard_map(
        local, mesh=mesh, in_specs=placed, out_specs=P("section", "expert", None), check_vma=False
    )
```
